32 devices in a mesh: shard: 8 (over y, x, core), rep: 4 (over z).
Axes of the slice: x: 2, y: 2, z: 4, core: 2. Of those that a mesh axis runs over, the one named last changes fastest.
Arguments:
- tokens: bfloat16 [4096, 1024], P(('shard', 'rep')), may hold values from -6 to 6
- lat_ids: int32 [4096], P(('shard', 'rep')), may hold values from 0 to 3, as said below
- cond: bfloat16 [4, 1024], replicated, may hold values from -6 to 6
- w_ada: bfloat16 [1024, 6144], P('shard'), may hold values from -0.1875 to 0.1875
- b_ada: bfloat16 [6144], P('shard'), may hold values from -3 to 3
- w_qkv: bfloat16 [1024, 3072], P('shard'), may hold values from -3 to 3
- b_qv: bfloat16 [2048], P('shard'), may hold values from -3 to 3
- w_out: bfloat16 [1024, 1024], P('shard'), may hold values from -3 to 3
- b_out: bfloat16 [1024], P('shard'), may hold values from -3 to 3
- w_fc1: bfloat16 [1024, 4096], P('shard'), may hold values from -0.1875 to 0.1875
- b_fc1: bfloat16 [4096], P('shard'), may hold values from -3 to 3
- w_fc2: bfloat16 [4096, 1024], P('shard'), may hold values from -0.09375 to 0.09375
- b_fc2: bfloat16 [1024], P('shard'), may hold values from -3 to 3
- cotangent: bfloat16 [4096, 1024], P(('shard', 'rep')), may hold values from -6 to 6
Outputs:
- output: bfloat16 [4096, 1024], P(('shard', 'rep'))
- grad_tokens: float32 [4096, 1024], P(('shard', 'rep'))
- grad_cond: float32 [4, 1024], P(None, 'shard')
- grad_w_ada: float32 [1024, 6144], P('shard')
- grad_b_ada: float32 [6144], P('shard')
- grad_w_qkv: float32 [1024, 3072], P('shard')
- grad_b_qv: float32 [2048], P('shard')
- grad_w_out: float32 [1024, 1024], P('shard')
- grad_b_out: float32 [1024], P('shard')
- grad_w_fc1: float32 [1024, 4096], P('shard')
- grad_b_fc1: float32 [4096], P('shard')
- grad_w_fc2: float32 [4096, 1024], P('shard')
- grad_b_fc2: float32 [1024], P('shard')
The draws below stay inside these ranges and needn't reach their ends.
Inputs may be any that keep to these rules, and one draw needn't show every extreme that they name: `lat_ids`: each aligned run of 1024 tokens shares one id, and the 4 runs carry different ids.
All inputs are finite; a program needn't handle non-finite values.
Results may differ from the reference program's by a relative error of at most 0.015.
The reference program's roundings to bfloat16 on the way count: a program that leaves them out, or rounds other values in their place, can miss the bound.
Values may be sent and summed in bfloat16 or wider, within the bound.
No kernel may reach another device: no remote copies, remote signals or barrier semaphores. Data moves between devices by JAX's collectives and lax.ppermute only.
A program may use at most 192 MiB of HBM per device.

```python
import jax
import jax.numpy as jnp
from jax import lax

D = 1024
H = 16
FF = 4096
LAT_TOK = 1024
TOKENS = 4096
LATENTS = 4


def draw_lat_ids(key, part):
    latent_order = jax.random.permutation(key, LATENTS).astype(jnp.int32)
    return jnp.repeat(latent_order, LAT_TOK, total_repeat_length=LATENTS * LAT_TOK)


def draw_w_qkv(key, part):
    keys = jax.random.split(jax.random.fold_in(key, 311), 1)
    scale = D ** (-0.5)
    return (jnp.clip(jax.random.normal(keys[0], (D, 3 * D), jnp.float32), -6.0, 6.0) * scale).astype(jnp.bfloat16)


def draw_tokens(key, part):
    keys = jax.random.split(jax.random.fold_in(key, 523), 1)
    return jnp.clip(jax.random.normal(keys[0], (TOKENS, D), jnp.float32), -6.0, 6.0).astype(jnp.bfloat16)


def spiked(values, stream_key, source, target, blocks, factor):
    def block_of(position):
        return (jnp.arange(values.shape[position]) // (values.shape[position] // blocks)).reshape((-1,) + (1,) * (values.ndim - 1 - position))

    one_side = jax.random.permutation(stream_key, blocks)[block_of(target)]
    far = (block_of(target) + blocks // 2) % blocks
    return jnp.where((block_of(source) == one_side) | (block_of(source) == far), factor * values, values)


def block_levels(stream_key, shape, pieces, low, largest):
    def one(dim, parts):
        heights = jax.random.uniform(jax.random.fold_in(jax.random.fold_in(stream_key, 6), dim), (parts,), jnp.float32, low / len(pieces), largest / len(pieces))
        return jnp.repeat(jnp.exp(heights), shape[dim] // parts).reshape((-1,) + (1,) * (len(shape) - dim - 1))

    loudness = one(*pieces[0])
    for cut in pieces[1:]:
        loudness = loudness * one(*cut)
    return loudness


def scatter_about(stream_key, dims, width, limit, shards=(), kind=jnp.bfloat16):
    entries = jax.random.normal(stream_key, dims, jnp.float32) * width
    if len(shards) > 0:
        entries = block_levels(stream_key, dims, shards, -0.22, 0.18) * entries
    return jnp.clip(entries, min=-limit, max=limit).astype(kind)


def bell_draw_with(own_key, shape, spread, limit, cuts, heavy, held_as=jnp.bfloat16):
    array = spread * jax.random.normal(own_key, shape, jnp.float32)
    if cuts:
        array = array * block_levels(own_key, shape, cuts, -0.22, 0.18)
    return jnp.clip(spiked(array, jax.random.fold_in(own_key, 3), *heavy), -limit, limit).astype(held_as)


def setup_inputs(seed: int = 0) -> dict:
    seeds = jax.random.split(jax.random.key(seed), 15)
    tokens = draw_tokens(jax.random.fold_in(seeds[14], 71), 0)
    lat_ids = draw_lat_ids(jax.random.fold_in(seeds[14], 71), 0)
    cond = scatter_about(seeds[2], (LATENTS, D), 1.0, 6.0)
    w_ada = scatter_about(seeds[3], (D, 6 * D), D ** -0.5, 0.1875, ((0, 8),))
    b_ada = scatter_about(seeds[4], (6 * D,), 0.5, 3.0, ((0, 8),))
    w_qkv = draw_w_qkv(jax.random.fold_in(seeds[14], 71), 0)
    b_qv = scatter_about(seeds[6], (2 * D,), 0.5, 3.0, ((0, 8),))
    w_out = scatter_about(seeds[7], (D, D), (D * 4 // LAT_TOK) ** -0.5, 3.0, ((0, 8),))
    b_out = scatter_about(seeds[8], (D,), 0.5, 3.0, ((0, 8),))
    w_fc1 = scatter_about(seeds[9], (D, FF), D ** -0.5, 0.1875, ((0, 8),))
    b_fc1 = scatter_about(seeds[10], (FF,), 0.5, 3.0, ((0, 8),))
    w_fc2 = scatter_about(seeds[11], (FF, D), FF ** -0.5, 0.09375, ((0, 8),))
    b_fc2 = scatter_about(seeds[12], (D,), 0.5, 3.0, ((0, 8),))
    cotangent = bell_draw_with(seeds[13], (TOKENS, D), 1.0, 6.0, ((0, 32),), (0, 1, 32, 2.75))
    return {"tokens": tokens, "lat_ids": lat_ids, "cond": cond, "w_ada": w_ada, "b_ada": b_ada, "w_qkv": w_qkv, "b_qv": b_qv, "w_out": w_out, "b_out": b_out, "w_fc1": w_fc1, "b_fc1": b_fc1, "w_fc2": w_fc2, "b_fc2": b_fc2, "cotangent": cotangent}


root_two_pi = 0.7978845608028654
cubic_term = 0.044715

def rounded(values):
    return lax.optimization_barrier(values.astype(jnp.bfloat16))

def layer_norm(values):
    centered = values - lax.optimization_barrier(jnp.mean(values, axis=-1, keepdims=True))
    factor = lax.rsqrt(lax.optimization_barrier(jnp.mean(centered * centered, axis=-1, keepdims=True)) + 1e-06)
    return (centered * factor, factor)

def norm_back(upstream, normed, factor):
    return factor * (upstream - lax.optimization_barrier(jnp.mean(upstream, axis=-1, keepdims=True)) - normed * lax.optimization_barrier(jnp.mean(upstream * normed, axis=-1, keepdims=True)))

def gelu_both(hidden):
    inner = root_two_pi * (hidden + cubic_term * hidden * hidden * hidden)
    tangent = jnp.tanh(inner)
    value = 0.5 * hidden * (1.0 + tangent)
    slope = 0.5 * (1.0 + tangent) + 0.5 * hidden * (1.0 - tangent * tangent) * root_two_pi * (1.0 + 3.0 * cubic_term * hidden * hidden)
    return (value, slope)

def split_heads(matrix, head_count):
    return matrix.astype(jnp.float32).reshape(matrix.shape[0], head_count, matrix.shape[1] // head_count)

def attend_forward(query, key_rows, value_rows, head_count):
    score_scale = (query.shape[1] // head_count) ** (-0.5)
    scores = jnp.einsum('qhd,khd->hqk', split_heads(query, head_count), split_heads(key_rows, head_count)) * score_scale
    row_peak = lax.optimization_barrier(jnp.max(scores, axis=-1, keepdims=True))
    log_total = row_peak + jnp.log(lax.optimization_barrier(jnp.sum(jnp.exp(scores - row_peak), axis=-1, keepdims=True)))
    soft_weights = rounded(jnp.exp(scores - log_total))
    attended = jnp.einsum('hqk,khd->qhd', soft_weights.astype(jnp.float32), split_heads(value_rows, head_count))
    return (rounded(attended.reshape(query.shape)), log_total)

def attend_backward(query, key_rows, value_rows, log_total, grad_attended, head_count):
    score_scale = (query.shape[1] // head_count) ** (-0.5)
    query_heads = split_heads(query, head_count)
    key_heads = split_heads(key_rows, head_count)
    value_heads = split_heads(value_rows, head_count)
    grad_heads = split_heads(grad_attended, head_count)
    scores = jnp.einsum('qhd,khd->hqk', query_heads, key_heads) * score_scale
    soft_exact = jnp.exp(scores - log_total)
    grad_soft = jnp.einsum('qhd,khd->hqk', grad_heads, value_heads)
    grad_scores = rounded(soft_exact * (grad_soft - lax.optimization_barrier(jnp.sum(soft_exact * grad_soft, axis=-1, keepdims=True))) * score_scale).astype(jnp.float32)
    grad_query = jnp.einsum('hqk,khd->qhd', grad_scores, key_heads).reshape(query.shape)
    grad_keys = jnp.einsum('hqk,qhd->khd', grad_scores, query_heads).reshape(key_rows.shape)
    soft_rounded = rounded(soft_exact).astype(jnp.float32)
    grad_values = jnp.einsum('hqk,qhd->khd', soft_rounded, grad_heads).reshape(value_rows.shape)
    return (grad_query, grad_keys, grad_values)

def reference(tokens, lat_ids, cond, w_ada, b_ada, w_qkv, b_qv, w_out, b_out, w_fc1, b_fc1, w_fc2, b_fc2, cotangent):
    model_width = tokens.shape[1]
    head_count = H
    cond_f = cond.astype(jnp.float32)
    sigmoid_cond = jax.nn.sigmoid(cond_f)
    silu_cond = rounded(cond_f * sigmoid_cond)
    mod_all = jnp.dot(silu_cond, w_ada, preferred_element_type=jnp.float32) + b_ada.astype(jnp.float32)
    first_ids = lat_ids.reshape(LATENTS, LAT_TOK)[:, 0].astype(jnp.int32)
    mod_rows = mod_all[first_ids]
    bias_qkv = jnp.concatenate([b_qv[:model_width], jnp.zeros((model_width,), jnp.bfloat16), b_qv[model_width:]]).astype(jnp.float32)
    bias_out = b_out.astype(jnp.float32)
    bias_one = b_fc1.astype(jnp.float32)
    bias_two = b_fc2.astype(jnp.float32)

    def one_latent(carry, item):
        token_rows, grad_rows, mod_row = item
        mod_parts = mod_row.reshape(6, model_width)
        token_f = token_rows.astype(jnp.float32)
        normed_one, factor_one = layer_norm(token_f)
        mixed_one = rounded(normed_one * (1.0 + mod_parts[1]) + mod_parts[0])
        qkv_rows = jnp.dot(mixed_one, w_qkv, preferred_element_type=jnp.float32) + bias_qkv
        query = rounded(qkv_rows[:, :model_width])
        key_rows = rounded(qkv_rows[:, model_width:2 * model_width])
        value_rows = rounded(qkv_rows[:, 2 * model_width:])
        attended, log_total = attend_forward(query, key_rows, value_rows, head_count)
        attn_out = jnp.dot(attended, w_out, preferred_element_type=jnp.float32) + bias_out
        resid_one = token_f + mod_parts[2] * attn_out
        normed_two, factor_two = layer_norm(resid_one)
        mixed_two = rounded(normed_two * (1.0 + mod_parts[4]) + mod_parts[3])
        hidden = jnp.dot(mixed_two, w_fc1, preferred_element_type=jnp.float32) + bias_one
        activ, slope = gelu_both(hidden)
        activ_b = rounded(activ)
        mlp_out = jnp.dot(activ_b, w_fc2, preferred_element_type=jnp.float32) + bias_two
        result = (resid_one + mod_parts[5] * mlp_out).astype(jnp.bfloat16)
        grad_out = grad_rows.astype(jnp.float32)
        grad_mlp = grad_out * mod_parts[5]
        grad_mlp_b = rounded(grad_mlp)
        grad_wtwo = jnp.dot(activ_b.T, grad_mlp_b, preferred_element_type=jnp.float32)
        grad_btwo = lax.optimization_barrier(jnp.sum(grad_mlp, axis=0))
        grad_hidden = jnp.dot(grad_mlp_b, w_fc2.T, preferred_element_type=jnp.float32) * slope
        grad_hidden_b = rounded(grad_hidden)
        grad_wone = jnp.dot(mixed_two.T, grad_hidden_b, preferred_element_type=jnp.float32)
        grad_bone = lax.optimization_barrier(jnp.sum(grad_hidden, axis=0))
        grad_mix_two = jnp.dot(grad_hidden_b, w_fc1.T, preferred_element_type=jnp.float32)
        grad_res_one = grad_out + norm_back(grad_mix_two * (1.0 + mod_parts[4]), normed_two, factor_two)
        grad_attn = grad_res_one * mod_parts[2]
        grad_attn_b = rounded(grad_attn)
        grad_wout = jnp.dot(attended.T, grad_attn_b, preferred_element_type=jnp.float32)
        grad_bout = lax.optimization_barrier(jnp.sum(grad_attn, axis=0))
        grad_attended = rounded(jnp.dot(grad_attn_b, w_out.T, preferred_element_type=jnp.float32))
        grad_query, grad_keys, grad_values = attend_backward(query, key_rows, value_rows, log_total, grad_attended, head_count)
        grad_qkv_b = jnp.concatenate([rounded(grad_query), rounded(grad_keys), rounded(grad_values)], axis=1)
        grad_wqkv = jnp.dot(mixed_one.T, grad_qkv_b, preferred_element_type=jnp.float32)
        grad_bqv = jnp.concatenate([lax.optimization_barrier(jnp.sum(grad_query, axis=0)), lax.optimization_barrier(jnp.sum(grad_values, axis=0))])
        grad_mix_one = jnp.dot(grad_qkv_b, w_qkv.T, preferred_element_type=jnp.float32)
        grad_input = grad_res_one + norm_back(grad_mix_one * (1.0 + mod_parts[1]), normed_one, factor_one)
        grad_mod_row = jnp.concatenate([lax.optimization_barrier(jnp.sum(grad_mix_one, axis=0)), lax.optimization_barrier(jnp.sum(grad_mix_one * normed_one, axis=0)), lax.optimization_barrier(jnp.sum(grad_res_one * attn_out, axis=0)), lax.optimization_barrier(jnp.sum(grad_mix_two, axis=0)), lax.optimization_barrier(jnp.sum(grad_mix_two * normed_two, axis=0)), lax.optimization_barrier(jnp.sum(grad_out * mlp_out, axis=0))])
        terms = (grad_wqkv, grad_bqv, grad_wout, grad_bout, grad_wone, grad_bone, grad_wtwo, grad_btwo)
        new_carry = tuple((total + term for total, term in zip(carry, terms)))
        return (new_carry, (result, grad_input, grad_mod_row))
    start_carry = (jnp.zeros(w_qkv.shape, jnp.float32), jnp.zeros(b_qv.shape, jnp.float32), jnp.zeros(w_out.shape, jnp.float32), jnp.zeros(b_out.shape, jnp.float32), jnp.zeros(w_fc1.shape, jnp.float32), jnp.zeros(b_fc1.shape, jnp.float32), jnp.zeros(w_fc2.shape, jnp.float32), jnp.zeros(b_fc2.shape, jnp.float32))
    stacked = (tokens.reshape(LATENTS, LAT_TOK, model_width), cotangent.reshape(LATENTS, LAT_TOK, model_width), mod_rows)
    totals, (results, grad_inputs, grad_mods) = lax.scan(one_latent, start_carry, stacked)
    grad_mod_all = jnp.zeros((LATENTS, 6 * model_width), jnp.float32).at[first_ids].set(grad_mods)
    grad_w_ada = jnp.dot(silu_cond.astype(jnp.float32).T, grad_mod_all, precision=lax.Precision.HIGHEST)
    grad_b_ada = lax.optimization_barrier(jnp.sum(grad_mod_all, axis=0))
    silu_slope = sigmoid_cond * (1.0 + cond_f * (1.0 - sigmoid_cond))
    grad_cond = jnp.dot(grad_mod_all, w_ada.astype(jnp.float32).T, precision=lax.Precision.HIGHEST) * silu_slope
    output = results.reshape(TOKENS, model_width)
    grad_tokens = grad_inputs.reshape(TOKENS, model_width)
    return (output, grad_tokens, grad_cond, grad_w_ada, grad_b_ada, totals[0], totals[1], totals[2], totals[3], totals[4], totals[5], totals[6], totals[7])
```

```python
import functools

import jax
import jax.numpy as jnp
from jax import lax
from jax.experimental import pallas as pl
from jax.experimental.pallas import tpu as pltpu
from jax.sharding import PartitionSpec as P

H = 16
LAT_TOK = 1024
AXES = ("shard", "rep")
F32 = jnp.float32
BF16 = jnp.bfloat16

root_two_pi = 0.7978845608028654
cubic_term = 0.044715


def log2(n):
    return n.bit_length() - 1


def swap(value, mask):
    count = lax.axis_size(AXES)
    return lax.ppermute(value, AXES, [(i, i ^ mask) for i in range(count)])


def layer_norm(values):
    centered = values - jnp.mean(values, axis=-1, keepdims=True)
    factor = lax.rsqrt(jnp.mean(centered * centered, axis=-1, keepdims=True) + 1e-06)
    return (centered * factor, factor)


def norm_back(upstream, normed, factor):
    return factor * (
        upstream
        - jnp.mean(upstream, axis=-1, keepdims=True)
        - normed * jnp.mean(upstream * normed, axis=-1, keepdims=True)
    )


def gelu_both(hidden):
    inner = root_two_pi * (hidden + cubic_term * hidden * hidden * hidden)
    tangent = jnp.tanh(inner)
    value = 0.5 * hidden * (1.0 + tangent)
    slope = 0.5 * (1.0 + tangent) + 0.5 * hidden * (1.0 - tangent * tangent) * root_two_pi * (
        1.0 + 3.0 * cubic_term * hidden * hidden
    )
    return (value, slope)


def dot(a, b):
    return jnp.dot(a, b, preferred_element_type=F32)


def dot_t(a, b):
    return lax.dot_general(a, b, (((1,), (1,)), ((), ())), preferred_element_type=F32)


def tdot(a, b):
    return lax.dot_general(a, b, (((0,), (0,)), ((), ())), preferred_element_type=F32)


def pick(stack, places):
    return jnp.concatenate([lax.dynamic_slice_in_dim(stack, p, 1, 0) for p in places], axis=0)


def after(value, *others):
    return lax.optimization_barrier((value, *others))[0]


def at(stack, place):
    return lax.dynamic_index_in_dim(stack, place, 0, keepdims=False)


VM = pl.BlockSpec(memory_space=pltpu.VMEM)
SM = pl.BlockSpec(memory_space=pltpu.SMEM)


def call(kernel, name, outs, *args, scratch=(), flops=0, exps=0, places=True):
    moved = sum(a.size * a.dtype.itemsize for a in args) + sum(
        functools.reduce(lambda x, y: x * y, shape, 1) * jnp.dtype(kind).itemsize for shape, kind in outs
    )
    return pl.pallas_call(
        kernel,
        in_specs=[SM] * places + [VM] * (len(args) - places),
        out_specs=[VM] * len(outs),
        out_shape=[jax.ShapeDtypeStruct(shape, kind) for shape, kind in outs],
        scratch_shapes=[pltpu.VMEM(shape, kind) for shape, kind in scratch],
        cost_estimate=pl.CostEstimate(flops=flops, bytes_accessed=moved, transcendentals=exps),
        compiler_params=pltpu.CompilerParams(vmem_limit_bytes=56 << 20),
        name=name,
    )(*args)


def rows_at(start, size):
    return pl.ds(pl.multiple_of(start, size), size)


def head_mask(rows, head, half):
    lane = lax.broadcasted_iota(jnp.int32, (rows, 2 * half), 1)
    return (lane >= head * half) & (lane < (head + 1) * half)


QB = 256
TB = 128


def prepare_kernel(place, cond, w_ada, narrow, tails, w_qkv, w_fc1, table, mine, theirs, low, high, *, latents, near, widths):
    s, j = place[0], place[1]
    width = w_qkv.shape[1] // 3
    cols = mine.shape[1] // 3
    n_ada, n_one, n_qv = widths
    table[:latents] = dot(cond[...], w_ada[...])
    table[latents:] = jnp.zeros((table.shape[0] - latents, table.shape[1]), F32)
    table[:latents, rows_at(s * n_ada, n_ada)] += narrow[:, :n_ada].astype(F32)
    first = slice(latents, latents + 1)
    table[first, rows_at(s * n_one, n_one)] = narrow[:, n_ada : n_ada + n_one].astype(F32)
    hidden_width = w_fc1.shape[1]
    table[first, rows_at(hidden_width + s * n_qv, n_qv)] = narrow[:, n_ada + n_one :].astype(F32)
    table[latents + 1 : latents + 2, : 2 * width] = tails[...]
    for p in range(3):
        mine[:, p * cols : (p + 1) * cols] = w_qkv[:, rows_at(p * width + j * cols, cols)]
        theirs[:, p * cols : (p + 1) * cols] = w_qkv[:, rows_at(p * width + (j ^ near) * cols, cols)]
    half = low.shape[0]
    size = low.shape[2]
    for k in range(2 * half):
        (low if k < half else high)[k % half] = w_fc1[:, rows_at((s ^ k) * size, size)]


def regroup_kernel(*refs, stay, go):
    stacks, (keep, send) = refs[:-2], refs[-2:]
    for chosen, out in ((stay, keep), (go, send)):
        for k, (stack, place) in enumerate(chosen):
            out[k] = stacks[stack][place]


def mod_row(place, table, part, width):
    return table[pl.ds(place[2], 1), part * width : (part + 1) * width]


def front_kernel(place, *refs, pieces, rows, scale, latents, hidden_width):
    low, high, cotangent, table = refs[:4]
    weights = refs[4 : 4 + pieces]
    mixed_ref, qkv_ref, nat_ref, lse_ref, mlp_ref, mlp_sum = refs[4 + pieces : 10 + pieces]
    sends = refs[10 + pieces :]
    s, j = place[0], place[1]
    width = low.shape[1]
    shift, gain, gate2 = (mod_row(place, table, i, width) for i in (0, 1, 5))
    grad_mlp = cotangent[...].astype(F32) * gate2
    mlp_ref[...] = grad_mlp.astype(BF16)
    mlp_sum[...] = jnp.broadcast_to(jnp.sum(grad_mlp, axis=0, keepdims=True), mlp_sum.shape)
    slim = weights[0].shape[2] // 3
    first = slice(latents, latents + 1)
    bias_q = table[first, rows_at(hidden_width + j * slim, slim)]
    bias_v = table[first, rows_at(hidden_width + width + j * slim, slim)]
    bias = jnp.concatenate([bias_q, jnp.zeros_like(bias_q), bias_v], axis=1)
    for q, piece in enumerate(weights):
        for c in range(2):
            nat_ref[rows_at((s ^ (c | (q << 1))) * rows, rows), :] = piece[c]
    half_tok = low.shape[0]

    for part, ref in enumerate((low, high)):

        @pl.loop(0, half_tok // TB)
        def _(b):
            normed, _ = layer_norm(ref[rows_at(b * TB, TB), :].astype(F32))
            mixed = (normed * (1.0 + gain) + shift).astype(BF16)
            target = rows_at(b * TB + part * half_tok, TB)
            mixed_ref[target, :] = mixed
            qkv_ref[target, :] = (dot(mixed, nat_ref[...]) + bias).astype(BF16)

    cols = nat_ref.shape[1] // 3
    half = cols // 2
    tokens = 2 * half_tok
    tops = len(sends)

    for b in range(tokens // QB):
        query = qkv_ref[b * QB : (b + 1) * QB, :cols]
        keys = qkv_ref[:, cols : 2 * cols]
        values = qkv_ref[:, 2 * cols :]
        total = None
        for head in range(2):
            q_h = jnp.where(head_mask(QB, head, half), query, jnp.zeros_like(query))
            v_h = jnp.where(head_mask(tokens, head, half), values, jnp.zeros_like(values))
            scores = dot_t(q_h, keys) * scale
            peak = jnp.max(scores, axis=-1, keepdims=True)
            soft = jnp.exp(scores - peak)
            norm = jnp.sum(soft, axis=-1, keepdims=True)
            part = dot((soft * (1.0 / norm)).astype(BF16), v_h)
            total = part if total is None else total + part
            lse = jnp.transpose(jnp.broadcast_to(peak + jnp.log(norm), (QB, 128)))
            lse_ref[4 * head : 4 * head + 4, b * QB : (b + 1) * QB] = lse[:4]
        total = total.astype(BF16)
        for t in range(QB // TB):
            k = b * (QB // TB) + t
            sends[k % tops][k // tops] = total[t * TB : (t + 1) * TB]


def middle_kernel(place, *refs, pieces, rows, span, latents):
    tops = span // 2
    got = refs[:tops]
    top, low, high, token, table = refs[tops : tops + 5]
    resid_ref, attn_ref, mixed_ref, att_ref, nat_ref = refs[tops + 5 :]
    s, j = place[0], place[1]
    width = token.shape[1]
    gate, shift, gain = (mod_row(place, table, i, width) for i in (2, 3, 4))
    for q in range(pieces):
        for c, ref in enumerate((low, high)):
            nat_ref[rows_at((s ^ (c | (q << 1))) * rows, rows), :] = ref[q * rows : (q + 1) * rows]
    cols = top.shape[2]
    for k in range(span):
        block = got[k][0] if k < tops else top[k - tops]
        att_ref[:, rows_at((j ^ k) * cols, cols)] = block
    attn = dot(att_ref[...], nat_ref[...]) + table[latents + 1 : latents + 2, :width]
    attn_ref[...] = attn
    resid = token[...].astype(F32) + gate * attn
    resid_ref[...] = resid
    normed, _ = layer_norm(resid)
    mixed_ref[...] = (normed * (1.0 + gain) + shift).astype(BF16)


def feed_kernel(
    place, low, high, grad_low, grad_high, stack_a, stack_b, two, table, activ_ref, hid_ref, near_ref, far_ref, sum_ref, one, *, ids, latents
):
    s = place[0]
    rows = stack_a.shape[1]
    for names, stack in zip(ids, (stack_a, stack_b)):
        for k, name in enumerate(names):
            one[rows_at((s ^ name) * rows, rows), :] = stack[k]
    size = stack_a.shape[2]
    bias = table[latents : latents + 1, rows_at(s * size, size)]
    sum_ref[...] = jnp.zeros_like(sum_ref)
    half_tok = low.shape[0]
    for part, (ref, grad) in enumerate(((low, grad_low), (high, grad_high))):

        @pl.loop(0, half_tok // QB)
        def _(b):
            here = rows_at(b * QB, QB)
            target = rows_at(b * QB + part * half_tok, QB)
            hidden = dot(ref[here, :], one[...]) + bias
            activ, slope = gelu_both(hidden)
            activ_ref[target, :] = activ.astype(BF16)
            grad_hidden = dot_t(grad[here, :], two[...]) * slope
            sum_ref[0:1, :] += jnp.sum(grad_hidden, axis=0, keepdims=True)
            grad_hidden = grad_hidden.astype(BF16)
            hid_ref[target, :] = grad_hidden
            back = dot_t(grad_hidden, one[...])
            if part == 0:
                near_ref[here, :] = back
            else:
                far_ref[here, :] = back.astype(BF16)


def split_kernel(near, far, own_ref, *sends):
    size = own_ref.shape[0]
    own_ref[...] = near[:size] + far[:size].astype(F32)
    for k, ref in enumerate(sends):
        part = slice((k + 1) * size, (k + 2) * size)
        ref[...] = (near[part] + far[part].astype(F32)).astype(BF16)


def split_sum(near, far, count):
    size = near.shape[0] // count
    wide = near.shape[1]
    return call(
        split_kernel,
        "split_sum",
        [((size, wide), F32)] + [((size, wide), BF16)] * (count - 1),
        near,
        far,
        places=False,
    )


def turn_kernel(place, *refs, pieces, span):
    parts = refs[:pieces]
    resid, cotangent, attn, table, nat = refs[pieces : pieces + 5]
    grad_ref, grad_b_ref, sum_ref = refs[pieces + 5 : pieces + 8]
    tops = span // 2
    sends = refs[pieces + 8 : pieces + 8 + tops]
    held = refs[pieces + 8 + tops]
    j = place[1]
    gate, gain = (mod_row(place, table, i, resid.shape[1]) for i in (2, 4))
    grad_mix = parts[0][...]
    for ref in parts[1:]:
        grad_mix = grad_mix + ref[...].astype(F32)
    normed, factor = layer_norm(resid[...])
    grad_res = cotangent[...].astype(F32) + norm_back(grad_mix * (1.0 + gain), normed, factor)
    grad_ref[...] = grad_res
    grad_attn = grad_res * gate
    grad_attn_b = grad_attn.astype(BF16)
    grad_b_ref[...] = grad_attn_b
    held[...] = dot_t(grad_attn_b, nat[...]).astype(BF16)
    cols = sends[0].shape[2]
    for k in range(span):
        sends[k % tops][k // tops] = held[:, rows_at((j ^ k) * cols, cols)]
    sum_ref[...] = jnp.concatenate(
        [
            jnp.sum(x, axis=0, keepdims=True)
            for x in (grad_res * attn[...], grad_mix, grad_mix * normed, grad_attn)
        ]
        + [jnp.zeros((4, grad_mix.shape[1]), F32)],
        axis=0,
    )


def back_kernel(*refs, span, scale):
    tops = span // 2
    got = refs[:tops]
    top, qkv, lse_ref, nat, low, high = refs[tops : tops + 6]
    out_ref, near_ref, far_ref, sum_ref, bias_ref, dk_acc, dv_acc, kt, grads = refs[tops + 6 :]
    cols = nat.shape[1] // 3
    half = cols // 2
    tokens = qkv.shape[0]
    for k in range(span):
        grads[k * TB : (k + 1) * TB] = got[k][0] if k < tops else top[k - tops]
    kt[...] = jnp.transpose(qkv[:, cols : 2 * cols].astype(F32)).astype(BF16)
    dk_acc[...] = jnp.zeros_like(dk_acc)
    dv_acc[...] = jnp.zeros_like(dv_acc)
    bias_ref[...] = jnp.zeros_like(bias_ref)
    sum_ref[...] = jnp.zeros_like(sum_ref)

    for b in range(tokens // QB):
        here = slice(b * QB, (b + 1) * QB)
        query = qkv[here, :cols]
        keys = qkv[:, cols : 2 * cols]
        values = qkv[:, 2 * cols :]
        grad = grads[here]
        pieces = []
        for head in range(2):
            mask = head_mask(QB, head, half)
            q_h = jnp.where(mask, query, jnp.zeros_like(query))
            do_h = jnp.where(mask, grad, jnp.zeros_like(grad))
            soft = jnp.exp(dot_t(keys, q_h) * scale - lse_ref[4 * head : 4 * head + 1, here])
            grad_soft = dot_t(values, do_h)
            mean = jnp.sum(soft * grad_soft, axis=0, keepdims=True)
            grad_scores = (soft * (grad_soft - mean) * scale).astype(BF16)
            dk_acc[...] += dot(grad_scores, q_h)
            dv_acc[...] += dot(soft.astype(BF16), do_h)
            pieces.append(dot(kt[head * half : (head + 1) * half, :], grad_scores))
        dq = jnp.transpose(jnp.concatenate(pieces, axis=0))
        out_ref[here, :cols] = dq.astype(BF16)
        bias_ref[0:1, :] += jnp.sum(dq, axis=0, keepdims=True)
    out_ref[:, cols : 2 * cols] = dk_acc[...].astype(BF16)
    out_ref[:, 2 * cols :] = dv_acc[...].astype(BF16)
    bias_ref[1:2, :] = jnp.sum(dv_acc[...], axis=0, keepdims=True)

    half_tok = tokens // 2
    for part, ref in enumerate((low, high)):

        @pl.loop(0, half_tok // TB)
        def _(b):
            here = rows_at(b * TB, TB)
            back = dot_t(out_ref[rows_at(b * TB + part * half_tok, TB), :], nat[...])
            normed, _ = layer_norm(ref[here, :].astype(F32))
            sum_ref[0:1, :] += jnp.sum(back, axis=0, keepdims=True)
            sum_ref[1:2, :] += jnp.sum(back * normed, axis=0, keepdims=True)
            if part == 0:
                near_ref[here, :] = back
            else:
                far_ref[here, :] = back.astype(BF16)


def order_kernel(place, blocks, low, high):
    half = low.shape[0]
    for k in range(2 * half):
        (low if k < half else high)[k % half] = blocks[place[0] ^ k]


def collect_kernel(place, low, high, out, *, ids):
    size = low.shape[2]
    for names, stack in zip(ids, (low, high)):
        for k, name in enumerate(names):
            out[:, rows_at((place[0] ^ name) * size, size)] = stack[k]


def heads_kernel(place, *refs):
    out_ref = refs[-1]
    pieces = refs[:-1]
    j = place[1]
    cols = pieces[0].shape[2] // 3
    width = out_ref.shape[1] // 3
    count = len(pieces)
    for k, ref in enumerate(pieces):
        for c in range(ref.shape[0]):
            for p in range(3):
                out_ref[:, rows_at(p * width + (j ^ (k + c * count)) * cols, cols)] = ref[
                    c, :, p * cols : (p + 1) * cols
                ].astype(F32)


def on_device(
    tokens,
    lat_ids,
    cond,
    w_ada,
    b_ada,
    w_qkv,
    b_qv,
    w_out,
    b_out,
    w_fc1,
    b_fc1,
    w_fc2,
    b_fc2,
    cotangent,
):
    own_tok, width = tokens.shape
    shards = lax.axis_size("shard")
    reps = lax.axis_size("rep")
    s = lax.axis_index("shard")
    r = lax.axis_index("rep")
    span = LAT_TOK // own_tok
    span_reps = min(reps, span)
    j = lax.rem(s * reps + r, span)
    latents = cond.shape[0]
    own_latent = lat_ids[0]
    place = jnp.stack([s, j, own_latent]).astype(jnp.int32)
    rows = w_qkv.shape[0]
    hidden_width = w_fc1.shape[1]
    slice_fc = hidden_width // shards
    cols = width // span
    scale = (width // H) ** (-0.5)

    core = reps
    both = span_reps < span
    shard_masks = [reps << b for b in range(log2(shards))]
    pieces = shards // 2
    wide = [(q << 1) * reps for q in range(pieces)]
    top = span // 2
    rep_bits = [1 << b for b in range(log2(reps))]

    def gather_rows(x):
        low = jnp.concatenate([x] + [swap(x, m) for m in wide[1:]], axis=0)
        return low, swap(low, core)

    def scatter_rows(near, far):
        own, *sends = split_sum(near, swap(far, core), pieces)
        return [own] + [swap(x, m) for x, m in zip(sends, wide[1:])]

    def total(parts):
        out = parts[0]
        for x in parts[1:]:
            out = out + x.astype(F32)
        return out

    low_tok = jnp.concatenate([tokens] + [swap(tokens, k) for k in range(1, top)], axis=0)
    high_tok = swap(low_tok, top)

    cond_f = cond.astype(F32)
    sigmoid_cond = jax.nn.sigmoid(cond_f)
    silu_cond = (cond_f * sigmoid_cond).astype(BF16)
    ada_rows = w_ada.shape[0]
    local_cond = lax.dynamic_slice_in_dim(silu_cond, s * ada_rows, ada_rows, 1)

    def spread(values):
        return jnp.where(jnp.arange(shards)[:, None] == s, values.astype(F32)[None, :], 0.0).reshape(-1)

    six = 6 * width
    narrow = jnp.concatenate([b_ada, b_fc1, b_qv])[None, :]
    tails = jnp.concatenate([spread(b_out), spread(b_fc2)])[None, :]
    half = shards // 2
    table, own_cols, core_cols, one_low, one_high = call(
        functools.partial(
            prepare_kernel,
            latents=latents,
            near=top if both else 0,
            widths=(b_ada.shape[0], b_fc1.shape[0], b_qv.shape[0]),
        ),
        "prepare",
        [
            ((latents + 2, six), F32),
            ((rows, 3 * cols), BF16),
            ((rows, 3 * cols), BF16),
            ((half, rows, slice_fc), BF16),
            ((half, rows, slice_fc), BF16),
        ],
        place,
        local_cond,
        w_ada,
        narrow,
        tails,
        w_qkv,
        w_fc1,
        flops=2 * latents * ada_rows * six,
    )
    for m in shard_masks:
        table = table + swap(table, m)

    pair = jnp.stack([own_cols, swap(core_cols, core)])
    qkv_pieces = [pair] + [swap(pair, m) for m in wide[1:]]

    lat_shape = (span * own_tok, width)
    tok_shape = (own_tok, width)
    mixed_one, qkv, qkv_cols, lse, grad_mlp_b, mlp_sums, *sends = call(
        functools.partial(
            front_kernel, pieces=pieces, rows=rows, scale=scale, latents=latents, hidden_width=hidden_width
        ),
        "front",
        [
            (lat_shape, BF16),
            ((lat_shape[0], 3 * cols), BF16),
            ((width, 3 * cols), BF16),
            ((8, lat_shape[0]), F32),
            (tok_shape, BF16),
            ((8, width), F32),
        ]
        + [((2, own_tok, cols), BF16)] * top,
        place,
        low_tok,
        high_tok,
        cotangent,
        table,
        *qkv_pieces,
        flops=2 * lat_shape[0] * width * 3 * cols + 8 * lat_shape[0] ** 2 * cols,
        exps=2 * lat_shape[0] ** 2,
    )

    out_low, out_high = gather_rows(after(w_out, table))

    def to_peers(sends):
        got = [sends[0]] + [swap(sends[k], k) for k in range(1, top)]
        return got, swap(jnp.stack([g[1] for g in got]), top)

    got, got_top = to_peers(sends)
    resid_one, attn_out, mixed_two, att, out_nat = call(
        functools.partial(middle_kernel, pieces=pieces, rows=rows, span=span, latents=latents),
        "middle",
        [(tok_shape, F32), (tok_shape, F32), (tok_shape, BF16), (tok_shape, BF16), ((width, width), BF16)],
        place,
        *got,
        got_top,
        out_low,
        out_high,
        tokens,
        table,
        flops=2 * own_tok * width * width,
    )

    def transpose_shards(low, high, ties):
        ids = [list(range(half)), list(range(half, shards))]
        low, high = low, swap(high, shard_masks[-1])
        for b, tie in zip(reversed(range(len(shard_masks) - 1)), ties):
            spots = [(i, p, name) for i, names in enumerate(ids) for p, name in enumerate(names)]
            stay = [x for x in spots if not x[2] >> b & 1]
            go = [x for x in spots if x[2] >> b & 1]
            block = low.shape
            low, send = call(
                functools.partial(regroup_kernel, stay=[x[:2] for x in stay], go=[x[:2] for x in go]),
                "regroup",
                [(block, low.dtype)] * 2,
                after(low, *tie),
                high,
                places=False,
            )
            high = swap(send, shard_masks[b])
            ids = [[x[2] for x in stay], [x[2] for x in go]]
        return low, high, ids

    steps = len(shard_masks) - 1
    one_a, one_b, one_ids = transpose_shards(
        one_low, after(one_high, out_low), [(mixed_one,)] + [(mixed_two,)] * (steps - 1)
    )
    grad_out = cotangent.astype(F32)
    grad_low, grad_high = gather_rows(grad_mlp_b)
    mix_low, mix_high = gather_rows(mixed_two)
    all_tok = shards * own_tok
    half_shape = (all_tok // 2, width)
    activ_b, grad_hidden_b, near, far, one_sums = call(
        functools.partial(feed_kernel, ids=one_ids, latents=latents),
        "feed",
        [
            ((all_tok, slice_fc), BF16),
            ((all_tok, slice_fc), BF16),
            (half_shape, F32),
            (half_shape, BF16),
            ((8, slice_fc), F32),
        ],
        place,
        mix_low,
        mix_high,
        grad_low,
        grad_high,
        one_a,
        one_b,
        w_fc2,
        table,
        scratch=[((width, slice_fc), BF16)],
        flops=6 * all_tok * width * slice_fc,
        exps=all_tok * slice_fc,
    )
    mix_parts = scatter_rows(near, far)

    grad_res_one, grad_attn_b, turn_sums, *sends = call(
        functools.partial(turn_kernel, pieces=pieces, span=span),
        "turn",
        [(tok_shape, F32), (tok_shape, BF16), ((8, width), F32)] + [((2, own_tok, cols), BF16)] * top,
        place,
        *mix_parts,
        resid_one,
        cotangent,
        attn_out,
        table,
        out_nat,
        scratch=[(tok_shape, BF16)],
        flops=2 * own_tok * width * width,
    )
    got, got_top = to_peers(sends)
    grad_qkv, near, far, late_sums, qv_sums = call(
        functools.partial(back_kernel, span=span, scale=scale),
        "back",
        [
            ((lat_shape[0], 3 * cols), BF16),
            ((lat_shape[0] // 2, width), F32),
            ((lat_shape[0] // 2, width), BF16),
            ((8, width), F32),
            ((8, cols), F32),
        ],
        *got,
        got_top,
        qkv,
        lse,
        qkv_cols,
        low_tok,
        high_tok,
        scratch=[
            ((lat_shape[0], cols), F32),
            ((lat_shape[0], cols), F32),
            ((cols, lat_shape[0]), BF16),
            ((lat_shape[0], cols), BF16),
        ],
        flops=20 * lat_shape[0] ** 2 * cols + 2 * lat_shape[0] * width * 3 * cols,
        exps=2 * lat_shape[0] ** 2,
        places=False,
    )
    own, *others = split_sum(near, swap(far, top), top)
    grad_mix_one = total([own] + [swap(x, k + 1) for k, x in enumerate(others)])
    own_mod = lax.dynamic_slice_in_dim(table, own_latent, 1, 0)
    scale1 = own_mod[:, width : 2 * width]
    gate2 = own_mod[:, 5 * width :]
    all_btwo = table[latents + 1, width : 2 * width]
    normed_one, factor_one = layer_norm(tokens.astype(F32))
    grad_tokens = grad_res_one + norm_back(grad_mix_one * (1.0 + scale1), normed_one, factor_one)

    mlp_part = dot(after(activ_b, grad_attn_b), w_fc2)
    mlp_near, mlp_far = jnp.split(mlp_part, 2, axis=0)
    mlp_out = total(scatter_rows(mlp_near, mlp_far.astype(BF16))) + all_btwo[None, :]
    output = (resid_one + gate2 * mlp_out).astype(BF16)

    def reduce_rep(x):
        for b, m in enumerate(rep_bits):
            bit = (r >> b) & 1
            view = x.reshape((x.shape[0] // 2, 2) + x.shape[1:])
            send = lax.dynamic_index_in_dim(view, 1 - bit, 1, keepdims=False).astype(BF16)
            keep = lax.dynamic_index_in_dim(view, bit, 1, keepdims=False)
            x = keep.astype(F32) + swap(send, m).astype(F32)
        return x[0]

    def gather_rep(block):
        x = block[None]
        for b, m in reversed(list(enumerate(rep_bits))):
            other = swap(x, m)
            bit = (r >> b) & 1
            x = jnp.stack([jnp.where(bit == 0, x, other), jnp.where(bit == 0, other, x)], axis=1)
            x = x.reshape((x.shape[0] * 2,) + x.shape[2:])
        return x

    all_grad = jnp.concatenate([grad_low, grad_high], axis=0)
    grad_wtwo = tdot(after(activ_b, mix_parts[0]), all_grad).astype(BF16).reshape(reps, slice_fc // reps, width)
    two_own = reduce_rep(grad_wtwo).astype(BF16)
    sum_wtwo = gather_rep(two_own).reshape(slice_fc, width).astype(F32)

    all_mix = jnp.concatenate([mix_low, mix_high], axis=0)
    one_rows = rows // reps
    grad_wone = tdot(all_mix, after(grad_hidden_b, grad_attn_b)).astype(BF16).reshape(shards, reps, one_rows, slice_fc)
    one_own = reduce_rep(grad_wone.transpose(1, 0, 2, 3)).astype(BF16)
    block = ((half, one_rows, slice_fc), BF16)
    low, high = call(order_kernel, "order", [block, block], place, one_own)
    low, high, ids = transpose_shards(low, high, [()] * steps)
    (one_own,) = call(
        functools.partial(collect_kernel, ids=ids), "collect", [((one_rows, hidden_width), BF16)], place, low, high
    )
    sum_wone = gather_rep(one_own).reshape(rows, hidden_width).astype(F32)

    wout = tdot(att, grad_attn_b).reshape(pieces, 2, rows, width)
    c = s & 1
    send = lax.dynamic_index_in_dim(wout, 1 - c, 1, keepdims=False).astype(BF16)
    wout = lax.dynamic_index_in_dim(wout, c, 1, keepdims=False) + swap(send, core).astype(F32)
    chip = s >> 1
    out_own = at(wout, chip)
    for q in range(1, pieces):
        out_own = out_own + swap(at(wout, chip ^ q).astype(BF16), wide[q]).astype(F32)
    out_own = reduce_rep(out_own.astype(BF16).reshape(reps, rows // reps, width))
    sum_wout = gather_rep(out_own.astype(BF16)).reshape(rows, width).astype(F32)

    wqkv = tdot(mixed_one, grad_qkv).reshape(pieces, 2, rows, 3 * cols)
    mine = at(wqkv, chip)
    for q in range(1, pieces):
        mine = mine + swap(at(wqkv, chip ^ q).astype(BF16), wide[q]).astype(F32)
    if both:
        for m in [span_reps << b for b in range(log2(reps // span_reps))]:
            mine = mine + swap(mine.astype(BF16), m).astype(F32)
        mine = mine.astype(BF16)
        mine = jnp.stack([at(mine, c), swap(at(mine, 1 - c), core)])
    else:
        mine = at(mine, c) + swap(at(mine, 1 - c).astype(BF16), core).astype(F32)
        for m in [span_reps << b for b in range(log2(reps // span_reps))]:
            mine = mine + swap(mine.astype(BF16), m).astype(F32)
        mine = mine.astype(BF16)[None]
    parts = [mine] + [swap(mine, k) for k in range(1, span_reps)]
    (sum_wqkv,) = call(heads_kernel, "heads", [((rows, 3 * width), F32)], place, *parts)

    small = jnp.concatenate(
        [
            late_sums[:2],
            turn_sums[:3],
            jnp.sum(grad_out * mlp_out, axis=0)[None],
            turn_sums[3:4],
            mlp_sums[:1],
            spread(one_sums[0]).reshape(-1, width),
            jnp.where((jnp.arange(span) == j)[None, :, None], qv_sums[:2, None, :], 0.0).reshape(2, width),
        ],
        axis=0,
    )
    bits = [1 << b for b in range(log2(shards * reps))]
    for m in bits[: log2(span)]:
        small = small + swap(small, m)
    is_own = (jnp.arange(latents) == own_latent)[:, None, None]
    small = jnp.concatenate([jnp.where(is_own, small[None, :6], 0.0).reshape(6 * latents, width), small[6:]], axis=0)
    for m in bits[log2(span) :]:
        small = small + swap(small, m)
    dmod = small[: 6 * latents].reshape(latents, six)
    rest = small[6 * latents :]

    grad_w_ada = jnp.dot(local_cond.astype(F32).T, dmod, precision=lax.Precision.HIGHEST)
    ada_cols = b_ada.shape[0]
    grad_b_ada = jnp.sum(lax.dynamic_slice_in_dim(dmod, s * ada_cols, ada_cols, 1), axis=0)
    local_sigmoid = lax.dynamic_slice_in_dim(sigmoid_cond, s * ada_rows, ada_rows, 1)
    local_raw = lax.dynamic_slice_in_dim(cond_f, s * ada_rows, ada_rows, 1)
    silu_slope = local_sigmoid * (1.0 + local_raw * (1.0 - local_sigmoid))
    grad_cond = jnp.dot(dmod, w_ada.astype(F32).T, precision=lax.Precision.HIGHEST) * silu_slope

    def own_part(vector, like):
        return lax.dynamic_slice_in_dim(vector, s * like.shape[0], like.shape[0], 0)

    fc_rows = hidden_width // width
    sum_bout = own_part(rest[0], b_out)
    sum_btwo = own_part(rest[1], b_fc2)
    sum_bone = own_part(rest[2 : 2 + fc_rows].reshape(-1), b_fc1)
    sum_bqv = own_part(rest[2 + fc_rows :].reshape(-1), b_qv)

    return (
        output,
        grad_tokens,
        grad_cond,
        grad_w_ada,
        grad_b_ada,
        sum_wqkv,
        sum_bqv,
        sum_wout,
        sum_bout,
        sum_wone,
        sum_bone,
        sum_wtwo,
        sum_btwo,
    )


def solution(mesh):
    placed = (
        P(("shard", "rep"), None),
        P(("shard", "rep")),
        P(),
        P("shard", None),
        P("shard"),
        P("shard", None),
        P("shard"),
        P("shard", None),
        P("shard"),
        P("shard", None),
        P("shard"),
        P("shard", None),
        P("shard"),
        P(("shard", "rep"), None),
    )
    return jax.shard_map(
        on_device,
        mesh=mesh,
        in_specs=placed,
        out_specs=(
            P(("shard", "rep"), None),
            P(("shard", "rep"), None),
            P(None, "shard"),
            P("shard", None),
            P("shard"),
            P("shard", None),
            P("shard"),
            P("shard", None),
            P("shard"),
            P("shard", None),
            P("shard"),
            P("shard", None),
            P("shard"),
        ),
        check_vma=False,
    )
```
